256 devices in a mesh: gx: 8 (over x, core), gy: 4 (over y), gz: 8 (over z).
Axes of the slice: x: 4, y: 4, z: 8, core: 2. Of those that a mesh axis runs over, the one named last changes fastest.
Arguments:
- right_side: float32 [128, 512, 512], P('gx', 'gz', 'gy'), may hold values from -8 to 8, as said below
- absorption: float32 [128, 512, 512], P('gx', 'gz', 'gy'), may hold values from 1e-05 to 1, as said below
Outputs:
- fine_iterate: float32 [128, 512, 512], P('gx', 'gz', 'gy')
- middle_iterate: float32 [64, 256, 256], P('gx', 'gz', 'gy')
- corrected_iterate: float32 [32, 128, 128], P('gx', 'gz', 'gy')
The draws below stay inside these ranges and needn't reach their ends.
Inputs may be any that keep to these rules, and one draw needn't show every extreme that they name: `right_side`: independent cell values, possibly with a smooth part added. `absorption`: positive at every cell.
All inputs are finite; a program needn't handle non-finite values.
Results may differ from the reference program's by a relative error of at most 0.0001.
Values sent between devices are 32-bit elements; how exact they have to be, the bound alone decides.
No kernel may reach another device: no remote copies, remote signals or barrier semaphores. Data moves between devices by JAX's collectives and lax.ppermute only.
A program may use at most 128 MiB of HBM per device.

```python
import math
import jax
import jax.numpy as jnp
from jax import lax

CX = 16
CY = 128
CZ = 64
DEGREE = 4
LEVELS = 3
BOTTOM_ITERS = 20
NX = 128
NY = 512
NZ = 512


def draw_right_side(key, part):
    noise = jnp.clip(jax.random.normal(key, (NX, NZ, NY), jnp.float32), -6.0, 6.0)
    return noise


def sponge_ramp(count, width):
    positions = jnp.arange(count, dtype=jnp.float32)
    distance = jnp.minimum(positions, count - 1.0 - positions) + 0.5
    return jnp.square(jnp.clip((width - distance) / width, 0.0, 1.0))


def draw_absorption(key, part):
    factor = jnp.exp(jax.random.uniform(key, (NX, NZ, NY), jnp.float32, math.log(0.5), math.log(2.0)))
    along_first = sponge_ramp(NX, CX * 1.0)
    along_second = sponge_ramp(NZ, CZ * 1.0)
    along_third = sponge_ramp(NY, CY * 1.0)
    profile = jnp.maximum(jnp.maximum(along_first[:, None, None], along_second[None, :, None]), along_third[None, None, :])
    return factor * (2e-05 + 0.49998 * profile)


def setup_inputs(seed: int = 0) -> dict:
    splits = jax.random.split(jax.random.key(seed), 3)
    return {
        "right_side": draw_right_side(jax.random.fold_in(splits[2], 71), 0),
        "absorption": draw_absorption(jax.random.fold_in(splits[2], 71), 0),
    }


smooth_low = 1.5
smooth_top = 12.0
absorb_top = 1.0
bottom_low = 0.008


def cheb_tables(count, lower, upper):
    theta = (upper + lower) / 2.0
    delta = (upper - lower) / 2.0
    sigma = theta / delta
    rho_value = 1.0 / sigma
    firsts = []
    seconds = []
    for turn_index in range(count - 1):
        rho_next = 1.0 / (2.0 * sigma - rho_value)
        firsts.append(rho_next * rho_value)
        seconds.append(2.0 * rho_next / delta)
        rho_value = rho_next
    return 1.0 / theta, firsts, seconds


def chebyshev(source, coefficient, count, lower, upper, operate):
    start_scale, firsts, seconds = cheb_tables(count, lower, upper)
    first_table = jnp.asarray(firsts, jnp.float32)
    second_table = jnp.asarray(seconds, jnp.float32)
    direction = source * start_scale

    def turn(turn_index, carry):
        iterate, direction, residual = carry
        residual = residual - operate(direction, coefficient)
        direction = first_table[turn_index] * direction + second_table[turn_index] * residual
        return (iterate + direction, direction, residual)

    iterate, direction, residual = lax.fori_loop(0, count - 1, turn, (direction, direction, source))
    return iterate


def neighbours(padded):
    return (padded[2:, 1:-1, 1:-1] + padded[:-2, 1:-1, 1:-1] + padded[1:-1, 2:, 1:-1]
            + padded[1:-1, :-2, 1:-1] + padded[1:-1, 1:-1, 2:] + padded[1:-1, 1:-1, :-2])


def global_operator(field, coefficient):
    return (6.0 + coefficient) * field - neighbours(jnp.pad(field, 1))


def restrict_four(field):
    first, second, third = field.shape
    blocks = field.reshape(first // 2, 2, second // 2, 2, third // 2, 2)
    return blocks.sum(axis=(1, 3, 5)) * 0.5


def prolong_axis(extended, axis):
    count = extended.shape[axis] - 2
    center = lax.slice_in_dim(extended, 1, count + 1, axis=axis)
    lower = lax.slice_in_dim(extended, 0, count, axis=axis)
    upper = lax.slice_in_dim(extended, 2, count + 2, axis=axis)
    even = 0.75 * center + 0.25 * lower
    odd = 0.75 * center + 0.25 * upper
    stacked = jnp.stack((even, odd), axis=axis + 1)
    shape = list(extended.shape)
    shape[axis] = 2 * count
    return stacked.reshape(shape)


def prolong(extended):
    for axis in range(3):
        extended = prolong_axis(extended, axis)
    return extended


def reference(right_side, absorption):
    source = right_side
    coefficient = absorption
    iterates = []
    for section in range(LEVELS):
        upper_bound = smooth_top + (4.0 ** section) * absorb_top
        iterate = chebyshev(source, coefficient, DEGREE + 1, smooth_low, upper_bound, global_operator)
        residual = source - global_operator(iterate, coefficient)
        iterates.append(iterate)
        source = restrict_four(residual)
        coefficient = restrict_four(coefficient)
    bottom_top = smooth_top + (4.0 ** LEVELS) * absorb_top
    correction = chebyshev(source, coefficient, BOTTOM_ITERS, bottom_low, bottom_top, global_operator)
    corrected = iterates[2] + prolong(jnp.pad(correction, 1))
    return iterates[0], iterates[1], corrected
```

```python
import jax
import jax.numpy as jnp
from jax import lax
from jax.experimental import pallas as pl
from jax.experimental.pallas import tpu as pltpu
from jax.sharding import PartitionSpec as P

DEGREE = 4
LEVELS = 3
BOTTOM_ITERS = 20

smooth_low = 1.5
smooth_top = 12.0
absorb_top = 1.0
bottom_low = 0.008

F32 = jnp.float32
HALO = 5
GROUPS = 25
LANES = 128


def cheb_tables(count, lower, upper):
    theta = (upper + lower) / 2.0
    delta = (upper - lower) / 2.0
    sigma = theta / delta
    rho_value = 1.0 / sigma
    firsts = []
    seconds = []
    for turn_index in range(count - 1):
        rho_next = 1.0 / (2.0 * sigma - rho_value)
        firsts.append(rho_next * rho_value)
        seconds.append(2.0 * rho_next / delta)
        rho_value = rho_next
    return (1.0 / theta, firsts, seconds)


def shift(value, axis, step):
    count = lax.axis_size(axis)
    return lax.ppermute(value, axis, [(i, (i + step) % count) for i in range(count)])


def flag(condition):
    return jnp.where(condition, 1.0, 0.0).astype(F32)


def edges(axis):
    index = lax.axis_index(axis)
    return flag(index > 0), flag(index < lax.axis_size(axis) - 1)


def lane_iota(rows):
    return lax.broadcasted_iota(jnp.int32, (rows, LANES), 1)


def row_iota(rows):
    return lax.broadcasted_iota(jnp.int32, (rows, LANES), 0)


def pair_sum(out_start, count):
    row = lax.broadcasted_iota(jnp.int32, (LANES, LANES), 0)
    column = lax.broadcasted_iota(jnp.int32, (LANES, LANES), 1) - out_start
    hit = (row // 2 == column) & (column >= 0) & (column < count)
    return jnp.where(hit, 0.5, 0.0).astype(F32)


def exact_dot(a, b):
    return jnp.dot(a, b, preferred_element_type=F32, precision=lax.Precision.HIGHEST)


def call(kernel, outs, scratch, *args):
    result = pl.pallas_call(
        kernel,
        out_shape=[jax.ShapeDtypeStruct(s, F32) for s in outs],
        in_specs=[pl.BlockSpec(memory_space=pltpu.VMEM)] * len(args),
        out_specs=[pl.BlockSpec(memory_space=pltpu.VMEM)] * len(outs),
        scratch_shapes=[pltpu.VMEM(s, F32) for s in scratch],
        compiler_params=pltpu.CompilerParams(vmem_limit_bytes=32 << 20),
    )(*args)
    return result


def step_rows(tiles, coef, sources, plane, start, rows, mask, coefs, b_scale, olds):
    lane = lane_iota(rows)
    here = pl.ds(start, rows)
    values = [t[plane, here, :] for t in tiles]
    right = [pltpu.roll(v, LANES - 1, 1) for v in values]
    left = [pltpu.roll(v, 1, 1) for v in values]
    if len(tiles) == 2:
        right = [
            jnp.where(lane == LANES - 1, right[1], right[0]),
            jnp.where(lane == LANES - 1, right[0], right[1]),
        ]
        left = [jnp.where(lane == 0, left[1], left[0]), jnp.where(lane == 0, left[0], left[1])]
    results = []
    for i, t in enumerate(tiles):
        around = (
            (right[i] + left[i])
            + (t[plane - 1, here, :] + t[plane + 1, here, :])
            + (t[plane, pl.ds(start - 1, rows), :] + t[plane, pl.ds(start + 1, rows), :])
        )
        if mask is not None:
            around = around * mask[i]
        inner = around - coef[i][plane, here, :] * values[i]
        of_value, of_source, of_old = coefs
        out = of_value * values[i] + b_scale * inner
        if of_source:
            out = out + of_source * sources[i][plane, here, :]
        if of_old:
            out = out + of_old * olds[i][plane, here, :]
        results.append(out)
    return results


def smooth(source, coef, bufs, planes, full_x, row_start, rows, masks, plane_ok, level_top, chunk):
    start_scale, firsts, seconds = cheb_tables(DEGREE + 1, smooth_low, level_top)
    now, other = source, None
    for k in range(DEGREE):
        a, b = firsts[k], seconds[k]
        target = bufs[k % 2]
        if k == 0:
            coefs = ((1.0 + a) * start_scale + b, 0.0, 0.0)
            b_here = b * start_scale
        elif k == 1:
            coefs = (1.0 + a, b - a * start_scale, 0.0)
            b_here = b
        else:
            coefs = (1.0 + a, b, -a)
            b_here = b
        low, high = (1, planes - 1) if full_x else (k + 1, planes - 1 - k)

        def body(plane, carry, now=now, target=target, coefs=coefs, b_here=b_here):
            scale = b_here * plane_ok(plane)
            for r in range(row_start, row_start + rows, chunk):
                part = [m[r - row_start : r - row_start + chunk, :] for m in masks]
                out = step_rows(
                    now, coef, source, plane, r, chunk, part, coefs, scale, target
                )
                for t, o in zip(target, out):
                    t[plane, pl.ds(r, chunk), :] = o
            return carry

        lax.fori_loop(low, high, body, 0)
        now = target
    return now


def residual_rows(tiles, coef, source, plane, start, rows):
    t = tiles[0]
    here = pl.ds(start, rows)
    value = t[plane, here, :]
    right = pltpu.roll(value, LANES - 1, 1)
    left = pltpu.roll(value, 1, 1)
    if len(tiles) == 2:
        lane = lane_iota(rows)
        far = tiles[1][plane, here, :]
        right = jnp.where(lane == LANES - 1, pltpu.roll(far, LANES - 1, 1), right)
        left = jnp.where(lane == 0, pltpu.roll(far, 1, 1), left)
    around = (
        (right + left)
        + (t[plane - 1, here, :] + t[plane + 1, here, :])
        + (t[plane, pl.ds(start - 1, rows), :] + t[plane, pl.ds(start + 1, rows), :])
    )
    return source[0][plane, here, :] - coef[0][plane, here, :] * value + around


def clear_pads(ref, planes, first, last):
    for p in range(planes):
        ref[p, 0:first, :] = jnp.zeros((first, LANES), F32)
        ref[p, last : last + 8, :] = jnp.zeros((8, LANES), F32)


S0_PLANES = list(range(1, 25))
C0_PLANES = list(range(2, 24))
STRIPS0 = [("s", p) for p in S0_PLANES] + [("c", p) for p in C0_PLANES]


def plane0(name, p, rs, ab, fl, fr):
    if name == "s":
        if p < 5:
            return fl, p
        if p < 21:
            return rs, p - 5
        return fr, p - 21
    if p < 5:
        return fl, 5 + p - 1
    if p < 21:
        return ab, p - 5
    return fr, 5 + p - 21


def z_strips_kernel(rs, ab, fl, fr, low, high):
    for i, (name, p) in enumerate(STRIPS0):
        ref, q = plane0(name, p, rs, ab, fl, fr)
        low[5 * i : 5 * i + 5, :] = ref[q, 0:5, :]
        high[5 * i : 5 * i + 5, :] = ref[q, 59:64, :]


def pack_lanes(strips, get, low, high, rows):
    lane = lane_iota(rows)
    for t in range((len(strips) + GROUPS - 1) // GROUPS):
        low_tile = jnp.zeros((rows, LANES), F32)
        high_tile = jnp.zeros((rows, LANES), F32)
        for g in range(GROUPS):
            i = t * GROUPS + g
            if i >= len(strips):
                break
            value, base, width = get(*strips[i])
            inside = (lane >= 5 * g) & (lane < 5 * g + 5)
            to_low = (5 * g - base) % LANES
            to_high = (5 * g - (base + width - 5)) % LANES
            a = pltpu.roll(value, to_low, 1) if to_low else value
            b = pltpu.roll(value, to_high, 1) if to_high else value
            low_tile = jnp.where(inside, a, low_tile)
            high_tile = jnp.where(inside, b, high_tile)
        low[t, :, :] = low_tile
        high[t, :, :] = high_tile


def build0_kernel(rs, ab, fl, fr, zl, zh, es, ec, low, high, c1, tmp, gathered):
    x_low, x_high = edges("gx")
    z_low, z_high = edges("gz")
    zero = jnp.zeros((16, LANES), F32)
    for p in range(26):
        ref, q = plane0("s", p, rs, ab, fl, fr)
        scale = x_low if p < 5 else (x_high if p > 20 else None)
        value = ref[q, :, :]
        es[p, 16:80, :] = value if scale is None else value * scale
        es[p, 0:16, :] = zero
        es[p, 80:96, :] = zero
        if p in S0_PLANES:
            i = STRIPS0.index(("s", p))
            below, above = zl[5 * i : 5 * i + 5, :], zh[5 * i : 5 * i + 5, :]
            below, above = below * z_low, above * z_high
            if scale is not None:
                below, above = below * scale, above * scale
            es[p, 11:16, :] = below
            es[p, 80:85, :] = above
    for p in range(26):
        if p in (0, 25):
            continue
        ref, q = plane0("c", p, rs, ab, fl, fr)
        ec[p, 16:80, :] = ref[q, :, :] + 6.0
        ec[p, 0:16, :] = zero
        ec[p, 80:96, :] = zero
        if p in C0_PLANES:
            i = STRIPS0.index(("c", p))
            ec[p, 11:16, :] = zl[5 * i : 5 * i + 5, :] + 6.0
            ec[p, 80:85, :] = zh[5 * i : 5 * i + 5, :] + 6.0

    def get(name, p):
        return (es if name == "s" else ec)[p, 8:88, :], 0, LANES

    pack_lanes(STRIPS0, get, low, high, 80)
    for i in range(8):
        tmp[...] = ab[2 * i, :, :] + ab[2 * i + 1, :, :]
        gathered[32 * i : 32 * i + 32, :] = (
            tmp[pl.ds(0, 32, stride=2), :] + tmp[pl.ds(1, 32, stride=2), :]
        )
    folded = exact_dot(gathered[...], pair_sum(64, 64))
    c1[...] = folded.reshape(8, 32, LANES)


def level0_kernel(es, ec, yl, yh, c1, it0, sc1, s1, cc1, a0, a1, b0, b1, tmp, gathered):
    x_low, x_high = edges("gx")
    y_low, y_high = edges("gy")
    z_low, z_high = edges("gz")
    lane = lane_iota(80)
    row = row_iota(80)
    ok_rows = jnp.where(row < 8, z_low, jnp.where(row >= 72, z_high, 1.0))
    ok_lanes = jnp.where(lane < 64, y_high, y_low)
    for ref, strips in ((s1, S0_PLANES), (cc1, C0_PLANES)):
        name = "s" if ref is s1 else "c"
        for p in range(26):
            if p not in strips:
                if ref is s1 or p not in (0, 25):
                    ref[p, :, :] = jnp.zeros((96, LANES), F32)
                continue
            i = STRIPS0.index((name, p))
            t, g = i // GROUPS, i % GROUPS
            from_low = pltpu.roll(yl[t, :, :], 123 - 5 * g, 1)
            from_high = pltpu.roll(yh[t, :, :], (LANES - 5 * g) % LANES, 1) if g else yh[t, :, :]
            value = jnp.where(lane < 5, from_high, jnp.where(lane >= 123, from_low, 0.0))
            if ref is s1:
                value = value * ok_lanes
            ref[p, 8:88, :] = value
            ref[p, 0:8, :] = jnp.zeros((8, LANES), F32)
            ref[p, 88:96, :] = jnp.zeros((8, LANES), F32)
    for ref in (a0, a1, b0, b1):
        clear_pads(ref, 26, 8, 88)

    def plane_ok(p):
        return jnp.where(p < 5, x_low, jnp.where(p > 20, x_high, 1.0))

    masks = [ok_rows, ok_rows * ok_lanes]
    last = smooth(
        [es, s1], [ec, cc1], [[a0, a1], [b0, b1]], 26, False, 8, 80, masks, plane_ok,
        smooth_top + absorb_top, 16,
    )

    def finish(i, carry):
        for half in range(2):
            p = 5 + 2 * i + half
            for r in range(16, 80, 16):
                it0[2 * i + half, r - 16 : r, :] = last[0][p, r : r + 16, :]
                value = residual_rows(last, [ec], [es], p, r, 16)
                if half == 0:
                    tmp[r - 16 : r, :] = value
                else:
                    tmp[r - 16 : r, :] = tmp[r - 16 : r, :] + value
        start = pl.multiple_of(32 * i, 32)
        gathered[pl.ds(start, 32), :] = (
            tmp[pl.ds(0, 32, stride=2), :] + tmp[pl.ds(1, 32, stride=2), :]
        )
        return carry

    lax.fori_loop(0, 8, finish, 0)
    folded = exact_dot(gathered[...], pair_sum(0, 64))
    sc1[...] = folded.reshape(8, 32, LANES) + c1[...]


STRIPS1 = [("s", p) for p in range(1, 17)] + [("c", p) for p in range(2, 16)]


def build1_kernel(sc, fl, fr, zl, zh, ext, low, high):
    for p in range(18):
        ref, q = (fl, p) if p < 5 else ((sc, p - 5) if p < 13 else (fr, p - 13))
        ext[p, 0:8, :] = zl[p, :, :]
        ext[p, 8:40, :] = ref[q, :, :]
        ext[p, 40:48, :] = zh[p, :, :]

    def get(name, p):
        return ext[p, :, :], (0 if name == "s" else 64), 64

    pack_lanes(STRIPS1, get, low, high, 48)


def level1_kernel(ext, yl, yh, it1, sc2, es, ec, a, b, tmp, gathered):
    x_low, x_high = edges("gx")
    y_low, y_high = edges("gy")
    z_low, z_high = edges("gz")
    lane = lane_iota(48)
    row = row_iota(48)
    ok_rows = jnp.where(row < 8, z_low, jnp.where(row >= 40, z_high, 1.0))
    ok_lanes = jnp.where(lane < 64, 1.0, jnp.where(lane < 96, y_high, y_low))
    ok = ok_rows * ok_lanes
    for p in range(18):
        value = ext[p, :, :]
        for name, ref in (("s", es), ("c", ec)):
            mine = value if name == "s" else pltpu.roll(value, 64, 1)
            if (name, p) in STRIPS1:
                i = STRIPS1.index((name, p))
                t, g = i // GROUPS, i % GROUPS
                from_low = pltpu.roll(yl[t, :, :], 123 - 5 * g, 1)
                from_high = pltpu.roll(yh[t, :, :], (64 - 5 * g) % LANES, 1)
                halo = jnp.where(
                    lane < 69, from_high, jnp.where(lane >= 123, from_low, 0.0)
                )
            else:
                halo = jnp.zeros((48, LANES), F32)
            full = jnp.where(lane < 64, mine, halo)
            if name == "s":
                full = full * ok
                if p < 5:
                    full = full * x_low
                if p > 12:
                    full = full * x_high
            else:
                full = full + 6.0
            ref[p, 8:56, :] = full
    clear_pads(es, 18, 8, 56)
    clear_pads(a, 18, 8, 56)
    clear_pads(b, 18, 8, 56)

    def plane_ok(p):
        return jnp.where(p < 5, x_low, jnp.where(p > 12, x_high, 1.0))

    last = smooth(
        [es], [ec], [[a], [b]], 18, False, 8, 48, [ok], plane_ok,
        smooth_top + 4.0 * absorb_top, 48,
    )
    for i in range(4):
        total = jnp.zeros((32, LANES), F32)
        for half in range(2):
            p = 5 + 2 * i + half
            it1[2 * i + half, :, :] = last[0][p, 16:48, :][:, 0:64]
            total = total + residual_rows(last, [ec], [es], p, 16, 32)
        tmp[...] = total
        gathered[16 * i : 16 * i + 16, :] = (
            tmp[pl.ds(0, 16, stride=2), :] + tmp[pl.ds(1, 16, stride=2), :]
        )
        tmp[...] = ext[5 + 2 * i, 8:40, :] + ext[6 + 2 * i, 8:40, :]
        gathered[64 + 16 * i : 80 + 16 * i, :] = (
            tmp[pl.ds(0, 16, stride=2), :] + tmp[pl.ds(1, 16, stride=2), :]
        )
    lane16 = lane_iota(16)
    folded = exact_dot(gathered[...], pair_sum(0, 64))
    for kind in range(2):
        total = jnp.zeros((16, LANES), F32)
        for i in range(4):
            value = folded[64 * kind + 16 * i : 64 * kind + 16 * i + 16, :]
            amount = (32 * i - 32 * kind) % LANES
            value = pltpu.roll(value, amount, 1) if amount else value
            total = jnp.where(lane16 // 32 == i, value, total)
        sc2[kind, :, :] = total


def level2_kernel(p0, p1, p2, p3, it2, piece, es, ec, a, b, tmp, gathered):
    gx = lax.axis_index("gx")
    y_low, y_high = edges("gy")
    z_low, z_high = edges("gz")
    chip, core = gx // 2, gx % 2
    lane = lane_iota(32)
    row = row_iota(32)
    ok_rows = jnp.where(row < 8, z_low, jnp.where(row >= 24, z_high, 1.0))
    ok_lanes = jnp.where(lane < 32, 1.0, jnp.where(lane < 80, y_high, y_low))
    ok = ok_rows * ok_lanes
    for ref in (es, a, b):
        for p in (0, 33):
            ref[p, :, :] = jnp.zeros((48, LANES), F32)
        clear_pads(ref, 34, 8, 40)
    for k, pieces in enumerate((p0, p1, p2, p3)):
        for j in range(2):
            owner = 2 * ((chip - k + 4) % 4) + (core + j) % 2
            for kind, ref in enumerate((es, ec)):
                mine = pieces[j, kind, :, :]
                halo = pieces[j, 2 + kind, :, :]
                for x in range(4):
                    first = pltpu.roll(mine, (LANES - 32 * x) % LANES, 1) if x else mine
                    above = pltpu.roll(halo, (32 - 32 * x) % LANES, 1) if x != 1 else halo
                    below = pltpu.roll(halo, (96 - 32 * x) % LANES, 1) if x != 3 else halo
                    full = jnp.where(
                        lane < 32,
                        first,
                        jnp.where(lane < 37, above, jnp.where(lane >= 123, below, 0.0)),
                    )
                    if kind == 0:
                        full = full * ok
                    ref[1 + 4 * owner + x, 8:40, :] = full if kind == 0 else full + 6.0
                if kind == 1:
                    total = mine[8:24, :] + pltpu.roll(mine[8:24, :], 96, 1)
                    tmp[...] = total
                    rows = tmp[pl.ds(0, 8, stride=2), :] + tmp[pl.ds(1, 8, stride=2), :]
                    at = pl.multiple_of(128 + 16 * owner, 16)
                    gathered[pl.ds(at, 8), :] = rows
                    gathered[pl.ds(at + 8, 8), :] = pltpu.roll(rows, 64, 1)

    last = smooth(
        [es], [ec], [[a], [b]], 34, True, 8, 32, [ok], lambda p: 1.0,
        smooth_top + 16.0 * absorb_top, 32,
    )
    for x in range(4):
        it2[x, :, :] = last[0][1 + 4 * gx + x, 16:32, :]

    def finish(i, carry):
        total = residual_rows(last, [ec], [es], 1 + 2 * i, 16, 16)
        total = total + residual_rows(last, [ec], [es], 2 + 2 * i, 16, 16)
        tmp[...] = total
        at = pl.multiple_of(8 * i, 8)
        gathered[pl.ds(at, 8), :] = (
            tmp[pl.ds(0, 8, stride=2), :] + tmp[pl.ds(1, 8, stride=2), :]
        )
        return carry

    lax.fori_loop(0, 16, finish, 0)
    lane8 = lane_iota(8)
    folded = exact_dot(gathered[...], pair_sum(0, 16))
    for kind in range(2):
        for half in range(2):
            total = jnp.zeros((8, LANES), F32)
            for x in range(8):
                at = 128 * kind + 8 * (8 * half + x)
                value = folded[at : at + 8, :]
                value = pltpu.roll(value, 16 * x, 1) if x else value
                total = jnp.where(lane8 // 16 == x, value, total)
            piece[kind, half, :, :] = total


def bottom_kernel(g0, g1, g2, g3, it2, out, s, c, a, b, window):
    gx, gy, gz = lax.axis_index("gx"), lax.axis_index("gy"), lax.axis_index("gz")
    lane8 = lane_iota(8)
    lane = lane_iota(64)
    for ref in (s, c, a, b):
        clear_pads(ref, 10, 8, 72)

    def unpack(slot, carry):
        z_owner = (gz - slot + 8) % 8
        at = pl.multiple_of(8 + 8 * z_owner, 8)
        for kind, ref in enumerate((s, c)):
            for x in range(8):
                total = jnp.zeros((8, LANES), F32)
                for m, pieces in enumerate((g0, g1, g2, g3)):
                    y_owner = (gy - m + 4) % 4
                    for half in range(2):
                        value = pieces[slot, kind, half, :, :]
                        start = 64 * half + 16 * y_owner
                        value = pltpu.roll(value, (start - 16 * x + LANES) % LANES, 1)
                        total = jnp.where(lane8 // 16 == 4 * half + y_owner, value, total)
                ref[1 + x, pl.ds(at, 8), :] = total if kind == 0 else total + 6.0
        return carry

    lax.fori_loop(0, 8, unpack, 0)
    zero = jnp.zeros((64, LANES), F32)

    def wrap(ref):
        ref[0, 8:72, :] = jnp.where(lane >= 64, pltpu.roll(ref[8, 8:72, :], 64, 1), 0.0)
        ref[9, 8:72, :] = jnp.where(lane < 64, pltpu.roll(ref[1, 8:72, :], 64, 1), 0.0)

    top = smooth_top + 4.0**LEVELS * absorb_top
    start_scale, firsts, seconds = cheb_tables(BOTTOM_ITERS, bottom_low, top)
    keep_right = jnp.where(lane % 64 == 63, 0.0, 1.0)
    keep_left = jnp.where(lane % 64 == 0, 0.0, 1.0)

    def update(now, target, of_value, of_source, of_old, scale):
        wrap(now)
        for p in range(1, 9):
            value = now[p, 8:72, :]
            around = (
                pltpu.roll(value, LANES - 1, 1) * keep_right
                + pltpu.roll(value, 1, 1) * keep_left
                + (now[p - 1, 8:72, :] + now[p + 1, 8:72, :])
                + (now[p, 7:71, :] + now[p, 9:73, :])
            )
            new = of_value * value + scale * (around - c[p, 8:72, :] * value)
            if of_source is not None:
                new = new + of_source * s[p, 8:72, :]
            if of_old is not None:
                new = new + of_old * target[p, 8:72, :]
            target[p, 8:72, :] = new

    f, g = firsts, seconds
    update(s, a, (1.0 + f[0]) * start_scale + g[0], None, None, g[0] * start_scale)
    update(a, b, 1.0 + f[1], g[1] - f[1] * start_scale, None, g[1])
    bufs = [a, b]
    for k in range(2, BOTTOM_ITERS - 1):
        update(bufs[(k + 1) % 2], bufs[k % 2], 1.0 + f[k], g[k], -f[k], g[k])
    last = bufs[(BOTTOM_ITERS - 2) % 2]
    row24 = row_iota(24)
    lane24 = lane_iota(24)
    low_row = pl.multiple_of(8 * gz, 8)
    rows_ok = ((row24 >= 8) | (gz > 0)) & ((row24 < 16) | (gz < 7))
    lanes_ok = ((lane24 >= 1) | (gy > 0)) & ((lane24 <= 16) | (gy < 3)) & (lane24 < 18)
    row = lax.broadcasted_iota(jnp.int32, (LANES, LANES), 0)
    column = lax.broadcasted_iota(jnp.int32, (LANES, LANES), 1)
    center = column // 2 + 1
    side = jnp.where(column % 2 == 0, center - 1, center + 1)
    spread = jnp.where(row == center, 0.75, jnp.where(row == side, 0.25, 0.0))
    spread = jnp.where(column < 32, spread, 0.0).astype(F32)
    for j in range(4):
        x = 2 * gx - 1 + j
        x_ok = (x >= 0) & (x < 16)
        xc = jnp.clip(x, 0, 15)
        value = last[1 + xc % 8, pl.ds(low_row, 24), :]
        amount = (2 * LANES - 64 * (xc // 8) - 16 * gy + 1) % LANES
        value = pltpu.roll(value, amount, 1)
        value = jnp.where(rows_ok & lanes_ok & x_ok, value, 0.0)
        window[24 * j : 24 * j + 24, :] = value
    wide = exact_dot(window[...], spread)
    planes = [wide[24 * j : 24 * j + 24, :] for j in range(4)]
    for i in range(4):
        base = i // 2 + 1
        near = base - 1 if i % 2 == 0 else base + 1
        mixed = 0.75 * planes[base] + 0.25 * planes[near]
        window[0:24, :] = mixed
        even = 0.75 * window[8:16, :] + 0.25 * window[7:15, :]
        odd = 0.75 * window[8:16, :] + 0.25 * window[9:17, :]
        window[pl.ds(32, 8, stride=2), :] = even
        window[pl.ds(33, 8, stride=2), :] = odd
        out[i, :, :] = (it2[i, :, :] + window[32:48, :])[:, 0:32]


def exchange(low, high, axis):
    return shift(high, axis, 1), shift(low, axis, -1)


def on_device(rs, ab):
    fl, fr = exchange(
        jnp.concatenate((rs[:5], ab[:4])), jnp.concatenate((rs[11:], ab[12:])), "gx"
    )
    low, high = call(z_strips_kernel, [(230, LANES)] * 2, [], rs, ab, fl, fr)
    zl, zh = exchange(low, high, "gz")
    es, ec, low, high, c1 = call(
        build0_kernel,
        [(26, 96, LANES)] * 2 + [(2, 80, LANES)] * 2 + [(8, 32, LANES)],
        [(64, LANES), (256, LANES)],
        rs, ab, fl, fr, zl, zh,
    )
    yl, yh = exchange(low, high, "gy")
    it0, sc1 = call(
        level0_kernel,
        [(16, 64, LANES), (8, 32, LANES)],
        [(26, 96, LANES)] * 6 + [(64, LANES), (256, LANES)],
        es, ec, yl, yh, c1,
    )
    fl, fr = exchange(sc1[:5], sc1[3:], "gx")
    ext = jnp.concatenate((fl, sc1, fr))
    zl, zh = exchange(ext[:, :8], ext[:, 24:], "gz")
    ext, low, high = call(
        build1_kernel,
        [(18, 48, LANES)] + [(2, 48, LANES)] * 2,
        [],
        sc1, fl, fr, zl, zh,
    )
    yl, yh = exchange(low, high, "gy")
    it1, sc2 = call(
        level1_kernel,
        [(8, 32, 64), (2, 16, LANES)],
        [(18, 64, LANES)] * 4 + [(32, LANES), (128, LANES)],
        ext, yl, yh,
    )
    zl, zh = exchange(sc2[:, :8], sc2[:, 8:], "gz")
    mine = jnp.concatenate((zl, sc2, zh), axis=1)
    yl, yh = exchange(mine, mine, "gy")
    part = lax.broadcasted_iota(jnp.int32, mine.shape, 2) % 32
    halo = jnp.where(part < 16, yh, yl)
    mine = jnp.concatenate((mine, halo))
    partner = lax.ppermute(mine, "gx", [(i, i ^ 1) for i in range(8)])
    pair = jnp.stack((mine, partner))
    pairs = [pair] + [shift(pair, "gx", 2 * k) for k in range(1, 4)]
    it2, piece = call(
        level2_kernel,
        [(4, 16, LANES), (2, 2, 8, LANES)],
        [(34, 48, LANES)] * 4 + [(16, LANES), (256, LANES)],
        *pairs,
    )
    column = jnp.stack([piece] + [shift(piece, "gz", k) for k in range(1, 8)])
    grids = [column] + [shift(column, "gy", k) for k in range(1, 4)]
    (corrected,) = call(
        bottom_kernel,
        [(4, 16, 32)],
        [(10, 80, LANES)] * 4 + [(96, LANES)],
        *grids, it2,
    )
    return it0, it1, corrected


def solution(mesh):
    placed = (P("gx", "gz", "gy"), P("gx", "gz", "gy"))
    return jax.shard_map(
        on_device,
        mesh=mesh,
        in_specs=placed,
        out_specs=(P("gx", "gz", "gy"), P("gx", "gz", "gy"), P("gx", "gz", "gy")),
        check_vma=False,
    )
```

```python
import jax
import jax.numpy as jnp
from jax import lax
from jax.experimental import pallas as pl
from jax.experimental.pallas import tpu as pltpu
from jax.sharding import PartitionSpec as P

DEGREE = 4
LEVELS = 3
BOTTOM_ITERS = 20

smooth_low = 1.5
smooth_top = 12.0
absorb_top = 1.0
bottom_low = 0.008

F32 = jnp.float32
HALO = 5
WIDE = 15
LANES = 128


def cheb_tables(count, lower, upper):
    theta = (upper + lower) / 2.0
    delta = (upper - lower) / 2.0
    sigma = theta / delta
    rho_value = 1.0 / sigma
    firsts = []
    seconds = []
    for turn_index in range(count - 1):
        rho_next = 1.0 / (2.0 * sigma - rho_value)
        firsts.append(rho_next * rho_value)
        seconds.append(2.0 * rho_next / delta)
        rho_value = rho_next
    return (1.0 / theta, firsts, seconds)


def shift(value, axis, step):
    count = lax.axis_size(axis)
    return lax.ppermute(value, axis, [(i, (i + step) % count) for i in range(count)])


def flag(condition):
    return jnp.where(condition, 1.0, 0.0).astype(F32)


def edges(axis):
    index = lax.axis_index(axis)
    return flag(index > 0), flag(index < lax.axis_size(axis) - 1)


def lane_iota(rows):
    return lax.broadcasted_iota(jnp.int32, (rows, LANES), 1)


def row_iota(rows):
    return lax.broadcasted_iota(jnp.int32, (rows, LANES), 0)


def pair_sum(out_start, count):
    row = lax.broadcasted_iota(jnp.int32, (LANES, LANES), 0)
    column = lax.broadcasted_iota(jnp.int32, (LANES, LANES), 1) - out_start
    hit = (row // 2 == column) & (column >= 0) & (column < count)
    return jnp.where(hit, 0.5, 0.0).astype(F32)


def exact_dot(a, b):
    return jnp.dot(a, b, preferred_element_type=F32, precision=lax.Precision.HIGHEST)


def call(kernel, outs, scratch, *args):
    result = pl.pallas_call(
        kernel,
        out_shape=[jax.ShapeDtypeStruct(s, F32) for s in outs],
        in_specs=[pl.BlockSpec(memory_space=pltpu.VMEM)] * len(args),
        out_specs=[pl.BlockSpec(memory_space=pltpu.VMEM)] * len(outs),
        scratch_shapes=[pltpu.VMEM(s, F32) for s in scratch],
        compiler_params=pltpu.CompilerParams(vmem_limit_bytes=32 << 20),
    )(*args)
    return result


def step_tables(level_top, count=DEGREE + 1, low=smooth_low):
    start_scale, firsts, seconds = cheb_tables(count, low, level_top)
    tables = []
    for k, (a, b) in enumerate(zip(firsts, seconds)):
        if k == 0:
            scale = b * start_scale
            tables.append((scale, ((1.0 + a) * start_scale + b) / scale, 0.0, 0.0))
        elif k == 1:
            tables.append((b, (1.0 + a) / b, (b - a * start_scale) / b, 0.0))
        else:
            tables.append((b, (1.0 + a) / b, 1.0, a))
    return tables


def combine(table, around, value, coef, source, old, scale):
    _, pull, lift, back = table
    inner = around - (coef - pull) * value
    if lift == 1.0:
        inner = inner + source()
    elif lift:
        inner = inner + lift * source()
    out = scale * inner
    if back:
        out = out - back * old()
    return out


def clear_pads(ref, planes, first, last):
    for p in range(planes):
        ref[p, 0:first, :] = jnp.zeros((first, LANES), F32)
        ref[p, last : last + 8, :] = jnp.zeros((8, LANES), F32)


def rolled(value, amount):
    amount = amount % LANES
    return pltpu.roll(value, amount, 1) if amount else value


def fold_rows(tmp, rows):
    return tmp[pl.ds(0, rows, stride=2), :] + tmp[pl.ds(1, rows, stride=2), :]


S0_PLANES = list(range(1, 25))
C0_PLANES = list(range(2, 24))
STRIPS0 = [("s", p) for p in S0_PLANES] + [("c", p) for p in C0_PLANES]


def strip_at(name, p):
    return 128 + 5 * STRIPS0.index((name, p))


def before_kernel(rs, ab, low, high, c1, tmp, gathered):
    lane = lane_iota(32)
    for i in range(8):
        tmp[...] = ab[2 * i, :, :] + ab[2 * i + 1, :, :]
        gathered[32 * i : 32 * i + 32, :] = fold_rows(tmp, 32)
    low[0:5, :, :] = rs[0:5, :, :]
    low[5:9, :, :] = ab[0:4, :, :]
    high[0:5, :, :] = rs[11:16, :, :]
    high[5:9, :, :] = ab[12:16, :, :]
    folded = exact_dot(gathered[...], pair_sum(0, 64))
    for j in range(4):
        first = folded[64 * j : 64 * j + 32, :]
        second = folded[64 * j + 32 : 64 * j + 64, :]
        pair = jnp.where(lane < 64, first, pltpu.roll(second, 64, 1))
        c1[j, :, :] = pair
        target = low if j < 2 else high
        target[9, 32 * (j % 2) : 32 * (j % 2) + 32, :] = pair


def plane0(name, p, rs, ab, fl, fr):
    if name == "s":
        if p < 5:
            return fl, p
        if p < 21:
            return rs, p - 5
        return fr, p - 21
    if p < 5:
        return fl, 5 + p - 1
    if p < 21:
        return ab, p - 5
    return fr, 5 + p - 21


def c1_pair(j, c1, fl, fr):
    if j < 2:
        return fl[9, 32 * j : 32 * j + 32, :]
    if j < 6:
        return c1[j - 2, :, :]
    return fr[9, 32 * (j - 6) : 32 * (j - 6) + 32, :]


def z_strips_kernel(rs, ab, c1, fl, fr, low, high):
    for j in range(8):
        pair = c1_pair(j, c1, fl, fr)
        low[16 * j : 16 * j + 16, :] = pair[0:16, :]
        high[16 * j : 16 * j + 16, :] = pair[16:32, :]
    for name, p in STRIPS0:
        ref, q = plane0(name, p, rs, ab, fl, fr)
        at = strip_at(name, p)
        low[at : at + 5, :] = ref[q, 0:5, :]
        high[at : at + 5, :] = ref[q, 59:64, :]


def wide_place(p):
    if 5 <= p < 13:
        return 0, WIDE * (p - 5), WIDE
    outer = [q for q in range(18) if q < 5 or q > 12]
    widths = [WIDE - (5 - q if q < 5 else q - 12) for q in outer]
    n = outer.index(p)
    return 1, sum(widths[:n]), widths[n]


def wide_pair(p):
    if p in (0, 17):
        return 8, p // 17
    return (p - 1) // 2, (p - 1) % 2


def pack_wide(pairs, planes, low, high, at):
    lane = lane_iota(64)
    for t in range(2):
        low_tile = jnp.zeros((64, LANES), F32)
        high_tile = jnp.zeros((64, LANES), F32)
        for p in planes:
            tile, start, width = wide_place(p)
            if tile != t:
                continue
            pair, half = wide_pair(p)
            value = pairs[pair, :, :]
            inside = (lane >= start) & (lane < start + width)
            low_tile = jnp.where(inside, rolled(value, start - 64 * half), low_tile)
            high_tile = jnp.where(
                inside, rolled(value, start - 64 * half - (64 - width)), high_tile
            )
        low[at + 64 * t : at + 64 * t + 64, :] = low_tile
        high[at + 64 * t : at + 64 * t + 64, :] = high_tile


def build0_kernel(rs, ab, c1, fl, fr, zl, zh, es, ec, low, high, c1e):
    x_low, x_high = edges("gx")
    z_low, z_high = edges("gz")
    zero = jnp.zeros((16, LANES), F32)
    for p in range(26):
        ref, q = plane0("s", p, rs, ab, fl, fr)
        scale = x_low if p < 5 else (x_high if p > 20 else None)
        value = ref[q, :, :]
        es[p, 16:80, :] = value if scale is None else value * scale
        es[p, 0:16, :] = zero
        es[p, 80:96, :] = zero
        if p in S0_PLANES:
            at = strip_at("s", p)
            below, above = zl[at : at + 5, :] * z_low, zh[at : at + 5, :] * z_high
            if scale is not None:
                below, above = below * scale, above * scale
            es[p, 11:16, :] = below
            es[p, 80:85, :] = above
    for p in range(1, 25):
        ref, q = plane0("c", p, rs, ab, fl, fr)
        ec[p, 16:80, :] = ref[q, :, :] + 6.0
        ec[p, 0:16, :] = zero
        ec[p, 80:96, :] = zero
        if p in C0_PLANES:
            at = strip_at("c", p)
            ec[p, 11:16, :] = zl[at : at + 5, :] + 6.0
            ec[p, 80:85, :] = zh[at : at + 5, :] + 6.0
    lane = lane_iota(16)
    for t, ref in enumerate((es, ec)):
        for r in range(0, 80, 16):
            low_tile = jnp.zeros((16, LANES), F32)
            high_tile = jnp.zeros((16, LANES), F32)
            for p in S0_PLANES:
                value = pltpu.roll(ref[p, 8 + r : 24 + r, :], 5 * p, 1)
                low_tile = jnp.where((lane >= 5 * p) & (lane < 5 * p + 5), value, low_tile)
                high_tile = jnp.where((lane >= 5 * p - 5) & (lane < 5 * p), value, high_tile)
            low[80 * t + r : 80 * t + r + 16, :] = low_tile
            high[80 * t + r : 80 * t + r + 16, :] = high_tile
    for j in range(8):
        c1e[j, 0:16, :] = zl[16 * j : 16 * j + 16, :]
        c1e[j, 16:48, :] = c1_pair(j, c1, fl, fr)
        c1e[j, 48:64, :] = zh[16 * j : 16 * j + 16, :]
    pack_wide(c1e, range(1, 17), low, high, 160)


def level0_kernel(
    es, ec, low_sent, high_sent, yl, yh, it0, s1, low, high,
    a0, b0, sl, sr, al, ar, bl, br, cl, cr, hz, tmp, gathered,
):
    x_low, x_high = edges("gx")
    y_low, y_high = edges("gy")
    z_low, z_high = edges("gz")
    lane = lane_iota(16)
    fifth = (lane * 52429) >> 18
    in_five = lane - 5 * fifth
    row = row_iota(16)
    first_rows = jnp.where(row < 8, z_low, 1.0)
    last_rows = jnp.where(row >= 8, z_high, 1.0)
    chunks = list(range(0, 80, 16))

    def row_mask(r):
        return first_rows if r == 0 else (last_rows if r == 64 else None)

    def plane_mask(p):
        return jnp.where(p < 5, x_low, jnp.where(p > 20, x_high, 1.0))

    left_ok = jnp.where(lane < 120, plane_mask(fifth + 1), 0.0) * y_low
    right_ok = jnp.where((lane >= 5) & (lane < 125), plane_mask(fifth), 0.0) * y_high

    def side_mask(r):
        rows_ok = row_mask(r)
        if rows_ok is None:
            return left_ok, right_ok
        return left_ok * rows_ok, right_ok * rows_ok

    for ref in (sl, sr, al, ar, bl, br):
        ref[0:8, :] = jnp.zeros((8, LANES), F32)
        ref[88:96, :] = jnp.zeros((8, LANES), F32)
    strips = []
    for r in chunks:
        left_mask, right_mask = side_mask(r)
        sl[8 + r : 24 + r, :] = yl[r : r + 16, :] * left_mask
        sr[8 + r : 24 + r, :] = yh[r : r + 16, :] * right_mask
        cl[r : r + 16, :] = yl[80 + r : 96 + r, :]
        cr[r : r + 16, :] = yh[80 + r : 96 + r, :]
        strips.append(
            jnp.where(in_five == 4, high_sent[r : r + 16, :], low_sent[r : r + 16, :])
        )
    clear_pads(a0, 26, 8, 88)
    clear_pads(b0, 26, 8, 88)

    def mix(left, right):
        for r in chunks:
            hz[r : r + 16, :] = jnp.where(
                in_five == 4,
                pltpu.roll(right[8 + r : 24 + r, :], LANES - 1, 1),
                pltpu.roll(left[8 + r : 24 + r, :], 1, 1),
            )

    def around_own(now, p, r, rows=16):
        here = 8 + r
        value = now[p, here : here + rows, :]
        beyond = pltpu.roll(hz[r : r + rows, :], LANES - 5 * p, 1)
        right = jnp.where(lane == LANES - 1, beyond, pltpu.roll(value, LANES - 1, 1))
        left = jnp.where(lane == 0, beyond, pltpu.roll(value, 1, 1))
        total = (
            (right + left)
            + (now[p - 1, here : here + rows, :] + now[p + 1, here : here + rows, :])
            + (now[p, here - 1 : here - 1 + rows, :] + now[p, here + 1 : here + 1 + rows, :])
        )
        return total, value

    tables = step_tables(smooth_top + absorb_top)
    now, left_now, right_now = es, sl, sr
    for k, table in enumerate(tables):
        target, left_to, right_to = ((a0, al, ar), (b0, bl, br))[k % 2]
        mix(left_now, right_now)
        for r, strip in zip(chunks, strips):
            here = 8 + r
            for side, mask, ref, to, source, coef in zip(
                range(2), side_mask(r), (left_now, right_now), (left_to, right_to), (sl, sr), (cl, cr)
            ):
                value = ref[here : here + 16, :]
                if side == 0:
                    right = pltpu.roll(jnp.where(in_five == 0, strip, value), LANES - 1, 1)
                    left = pltpu.roll(value, 1, 1)
                else:
                    right = pltpu.roll(value, LANES - 1, 1)
                    left = pltpu.roll(jnp.where(in_five == 4, strip, value), 1, 1)
                total = (
                    (right + left)
                    + (pltpu.roll(value, 5, 1) + pltpu.roll(value, LANES - 5, 1))
                    + (ref[here - 1 : here + 15, :] + ref[here + 1 : here + 17, :])
                )
                to[here : here + 16, :] = combine(
                    table, total, value, coef[r : r + 16, :],
                    lambda: source[here : here + 16, :],
                    lambda: to[here : here + 16, :],
                    mask * table[0],
                )

        trips = 3 if k == 0 else 2
        each = (24 - 2 * k) // trips

        def body(i, carry, now=now, target=target, table=table, k=k, each=each):
            carry = list(carry)
            for q in range(each):
                p = k + 1 + each * i + q
                scale = table[0] * plane_mask(p)
                for r in chunks:
                    total, value = around_own(now, p, r)
                    here = 8 + r
                    rows_ok = row_mask(r)
                    new = combine(
                        table, total, value, ec[p, here : here + 16, :],
                        lambda: es[p, here : here + 16, :],
                        lambda: target[p, here : here + 16, :],
                        scale if rows_ok is None else scale * rows_ok,
                    )
                    target[p, here : here + 16, :] = new
            for q in range(each if k < DEGREE - 1 else 0):
                p = k + 1 + each * i + q
                kept = (lane == 5 * p) | (lane == 5 * p - 1)
                for n, r in enumerate(chunks):
                    edge = pltpu.roll(target[p, 8 + r : 24 + r, :], 5 * p, 1)
                    carry[n] = jnp.where(kept, edge, carry[n])
            return tuple(carry)

        empty = tuple(jnp.zeros((16, LANES), F32) for _ in chunks)
        strips = lax.fori_loop(0, trips, body, empty)
        now, left_now, right_now = target, left_to, right_to
    mix(left_now, right_now)

    def finish(i, carry):
        for r in range(8, 72, 16):
            total = None
            for half in range(2):
                p = 5 + 2 * i + half
                around, value = around_own(now, p, r)
                it0[2 * i + half, r - 8 : r + 8, :] = value
                here = 8 + r
                left_over = (
                    es[p, here : here + 16, :] - ec[p, here : here + 16, :] * value + around
                )
                total = left_over if total is None else total + left_over
            tmp[r - 8 : r + 8, :] = total
        gathered[pl.ds(pl.multiple_of(32 * i, 32), 32), :] = fold_rows(tmp, 32)
        return carry

    lax.fori_loop(0, 8, finish, 0)
    folded = exact_dot(gathered[...], pair_sum(0, 64))
    lane32 = lane_iota(32)
    for j in range(4):
        first = folded[64 * j : 64 * j + 32, :]
        second = folded[64 * j + 32 : 64 * j + 64, :]
        pair = jnp.where(lane32 < 64, first, pltpu.roll(second, 64, 1))
        s1[j, :, :] = pair
        if j < 3:
            low[j, :, :] = pair
        if j > 0:
            high[j - 1, :, :] = pair


def s1_pair(j, s1, fl, fr):
    if j < 2:
        return fl[1 + j, :, :]
    if j < 6:
        return s1[j - 2, :, :]
    if j < 8:
        return fr[j - 6, :, :]
    return jnp.where(
        lane_iota(32) < 64, pltpu.roll(fl[0, :, :], 64, 1), pltpu.roll(fr[2, :, :], 64, 1)
    )


def z_strips1_kernel(s1, fl, fr, low, high):
    for j in range(9):
        pair = s1_pair(j, s1, fl, fr)
        low[16 * j : 16 * j + 16, :] = pair[0:16, :]
        high[16 * j : 16 * j + 16, :] = pair[16:32, :]


def build1_kernel(s1, fl, fr, zl, zh, ext, low, high):
    for j in range(9):
        ext[j, 0:16, :] = zl[16 * j : 16 * j + 16, :]
        ext[j, 16:48, :] = s1_pair(j, s1, fl, fr)
        ext[j, 48:64, :] = zh[16 * j : 16 * j + 16, :]
    pack_wide(ext, range(18), low, high, 0)


def level1_kernel(
    ext, yl, yh, c1e, low0, high0, it1, piece, es, ec, a, b, tmp, gathered
):
    x_low, x_high = edges("gx")
    y_low, y_high = edges("gy")
    z_low, z_high = edges("gz")
    lane = lane_iota(64)
    row = row_iota(64)
    ok_rows = jnp.where(row < 16, z_low, jnp.where(row >= 48, z_high, 1.0))
    ok_lanes = jnp.where(lane < 64, 1.0, jnp.where(lane < 96, y_high, y_low))
    ok = ok_rows * ok_lanes
    for p in range(18):
        t, at_lane, width = wide_place(p)
        pair, half = wide_pair(p)
        for kind, (pairs, below, above, base) in enumerate(
            ((ext, yl, yh, 0), (c1e, low0, high0, 160))
        ):
            if kind == 1 and p in (0, 17):
                continue
            mine = rolled(pairs[pair, :, :], 64 * half)
            at = base + 64 * t
            from_low = rolled(below[at : at + 64, :], LANES - width - at_lane)
            from_high = rolled(above[at : at + 64, :], 64 - at_lane)
            full = jnp.where(
                lane < 64,
                mine,
                jnp.where(
                    lane < 64 + width,
                    from_high,
                    jnp.where(lane >= LANES - width, from_low, 0.0),
                ),
            )
            if kind == 0:
                full = full * ok
                if p < 5:
                    full = full * x_low
                if p > 12:
                    full = full * x_high
                es[p, 8:72, :] = full
            else:
                ec[p, 8:72, :] = full + 6.0
                if 5 <= p < 13:
                    if p % 2 == 1:
                        tmp[...] = full
                    else:
                        tmp[...] = tmp[...] + full
                        j = (p - 5) // 2
                        gathered[128 + 32 * j : 160 + 32 * j, :] = fold_rows(tmp, 32)
    lane32 = lane_iota(32)
    clear_pads(es, 18, 8, 72)
    clear_pads(a, 18, 8, 72)
    clear_pads(b, 18, 8, 72)

    def around_of(now, p, start, rows):
        here = slice(start, start + rows)
        value = now[p, here, :]
        total = (
            (pltpu.roll(value, LANES - 1, 1) + pltpu.roll(value, 1, 1))
            + (now[p - 1, here, :] + now[p + 1, here, :])
            + (now[p, start - 1 : start - 1 + rows, :] + now[p, start + 1 : start + 1 + rows, :])
        )
        return total, value

    now = es
    for k, table in enumerate(step_tables(smooth_top + 4.0 * absorb_top)):
        target = (a, b)[k % 2]

        trips = 4 if k == 0 else 2
        each = (16 - 2 * k) // trips

        def body(i, carry, now=now, target=target, table=table, k=k, each=each):
            for q in range(each):
                p = k + 1 + each * i + q
                scale = table[0] * jnp.where(p < 5, x_low, jnp.where(p > 12, x_high, 1.0))
                for start in range(8, 72, 16):
                    here = slice(start, start + 16)
                    total, value = around_of(now, p, start, 16)
                    target[p, here, :] = combine(
                        table, total, value, ec[p, here, :],
                        lambda: es[p, here, :],
                        lambda: target[p, here, :],
                        ok[start - 8 : start + 8, :] * scale,
                    )
            return carry

        lax.fori_loop(0, trips, body, 0)
        now = target
    for i in range(4):
        for start in range(8, 72, 16):
            total = None
            for half in range(2):
                p = 5 + 2 * i + half
                around, value = around_of(now, p, start, 16)
                here = slice(start, start + 16)
                left_over = es[p, here, :] - ec[p, here, :] * value + around
                total = left_over if total is None else total + left_over
                if 24 <= start < 56:
                    it1[2 * i + half, start - 24 : start - 8, :] = value[:, 0:64]
            tmp[start - 8 : start + 8, :] = total
        gathered[32 * i : 32 * i + 32, :] = fold_rows(tmp, 32)
    j = lax.broadcasted_iota(jnp.int32, (LANES, LANES), 0)
    column = lax.broadcasted_iota(jnp.int32, (LANES, LANES), 1)
    goes_to = jnp.where(j < 74, j // 2 + 5, jnp.where(j >= 118, (j - 118) // 2, -1))
    folded = exact_dot(gathered[...], jnp.where(goes_to == column, 0.5, 0.0).astype(F32))
    for kind in range(2):
        for half in range(2):
            at = 128 * kind + 64 * half
            first, second = folded[at : at + 32, :], folded[at + 32 : at + 64, :]
            piece[2 * kind + half, :, :] = jnp.where(lane32 < 64, first, pltpu.roll(second, 64, 1))


def level2_kernel(mine, other, it2, piece, es, ec, a, b, tmp, gathered):
    gx = lax.axis_index("gx")
    y_low, y_high = edges("gy")
    z_low, z_high = edges("gz")
    chip, core = gx // 2, gx % 2
    lane = lane_iota(32)
    row = row_iota(32)
    place = lane % 64
    ok_rows = jnp.where(row < 8, z_low, jnp.where(row >= 24, z_high, 1.0))
    ok_lanes = jnp.where(
        place < 5, y_low, jnp.where(place < 37, 1.0, jnp.where(place < 42, y_high, 0.0))
    )
    ok = ok_rows * ok_lanes
    for ref in (es, a, b):
        for p in (0, 17):
            ref[p, :, :] = jnp.zeros((48, LANES), F32)
        clear_pads(ref, 18, 8, 40)
    for j, pieces in enumerate((mine, other)):
        for k in range(4):
            owner = 2 * ((chip - k + 4) % 4) + (core + j) % 2
            for t in range(2):
                tile = 2 * owner + t
                es[1 + tile, 8:40, :] = pieces[k, t, :, :] * ok
                value = pieces[k, 2 + t, :, :]
                ec[1 + tile, 8:40, :] = value + 6.0
                tmp[...] = value[8:24, :]
                gathered[pl.ds(pl.multiple_of(128 + 8 * tile, 8), 8), :] = fold_rows(tmp, 8)

    def around_of(now, p, start, rows):
        here = slice(start, start + rows)
        upper_half = lane_iota(rows) >= 64
        value = now[p, here, :]
        ahead = pltpu.roll(jnp.where(upper_half, value, now[p + 1, here, :]), 64, 1)
        behind = pltpu.roll(jnp.where(upper_half, now[p - 1, here, :], value), 64, 1)
        total = (
            (pltpu.roll(value, LANES - 1, 1) + pltpu.roll(value, 1, 1))
            + (ahead + behind)
            + (now[p, start - 1 : start - 1 + rows, :] + now[p, start + 1 : start + 1 + rows, :])
        )
        return total, value

    now = es
    for k, table in enumerate(step_tables(smooth_top + 16.0 * absorb_top)):
        target = (a, b)[k % 2]
        ok_scaled = ok * table[0]

        for p in range(1, 17):
            for start in (8, 24):
                here = slice(start, start + 16)
                total, value = around_of(now, p, start, 16)
                target[p, here, :] = combine(
                    table, total, value, ec[p, here, :],
                    lambda: es[p, here, :],
                    lambda: target[p, here, :],
                    ok_scaled[start - 8 : start + 8, :],
                )
        now = target
    for t in range(2):
        it2[t, :, :] = now[1 + 2 * gx + t, 16:32, :]
    for t in range(16):
        around, value = around_of(now, 1 + t, 16, 16)
        tmp[...] = es[1 + t, 16:32, :] - ec[1 + t, 16:32, :] * value + around
        gathered[8 * t : 8 * t + 8, :] = fold_rows(tmp, 8)
    j = lax.broadcasted_iota(jnp.int32, (LANES, LANES), 0) % 64
    column = lax.broadcasted_iota(jnp.int32, (LANES, LANES), 1)
    goes_to = jnp.where((j >= 5) & (j < 37), (j - 5) // 2, -1)
    folded = exact_dot(gathered[...], jnp.where(goes_to == column, 0.5, 0.0).astype(F32))
    lane8 = lane_iota(8)
    for half in range(2):
        total = jnp.zeros((8, LANES), F32)
        for x in range(8):
            at = 8 * (8 * half + x)
            value = jnp.where(core == 0, folded[at : at + 8, :], folded[128 + at : 136 + at, :])
            total = jnp.where(lane8 // 16 == x, rolled(value, 16 * x), total)
        piece[half, :, :] = total


Z_SLOTS = (0, -1, 1, -3, -4, -2, 3, 2)


def bottom_kernel(mine, other, it2, out, s, c, a, b, window):
    gx, gy, gz = lax.axis_index("gx"), lax.axis_index("gy"), lax.axis_index("gz")
    core = gx % 2
    lane8 = lane_iota(8)
    lane = lane_iota(64)
    for ref in (s, a, b):
        clear_pads(ref, 10, 8, 72)

    def unpack(slot, carry):
        offset = jnp.int32(0)
        for n, o in enumerate(Z_SLOTS):
            offset = jnp.where(slot == n, o, offset)
        z_owner = (gz + offset + 8) % 8
        at = pl.multiple_of(8 + 8 * z_owner, 8)
        for kind, ref in enumerate((s, c)):
            for x in range(8):
                total = jnp.zeros((8, LANES), F32)
                for m in range(4):
                    y_owner = (gy - m + 4) % 4
                    for half in range(2):
                        value = jnp.where(
                            core == kind, mine[m, slot, half, :, :], other[m, slot, half, :, :]
                        )
                        start = 64 * half + 16 * y_owner
                        value = pltpu.roll(value, (start - 16 * x + LANES) % LANES, 1)
                        total = jnp.where(lane8 // 16 == 4 * half + y_owner, value, total)
                ref[1 + x, pl.ds(at, 8), :] = total if kind == 0 else total + 6.0
        return carry

    lax.fori_loop(0, 8, unpack, 0)

    def wrap(ref):
        ref[0, 8:72, :] = jnp.where(lane >= 64, pltpu.roll(ref[8, 8:72, :], 64, 1), 0.0)
        ref[9, 8:72, :] = jnp.where(lane < 64, pltpu.roll(ref[1, 8:72, :], 64, 1), 0.0)

    top = smooth_top + 4.0**LEVELS * absorb_top
    lane16 = lane_iota(16)
    keep_right = jnp.where(lane16 % 64 == 63, 0.0, 1.0)
    keep_left = jnp.where(lane16 % 64 == 0, 0.0, 1.0)
    now = s
    for k, table in enumerate(step_tables(top, BOTTOM_ITERS, bottom_low)):
        target = (a, b)[k % 2]
        for p in (4, 5, 3, 6, 2, 7, 1, 8):
            if p == 1:
                wrap(now)
            for start in range(8, 72, 16):
                here = slice(start, start + 16)
                value = now[p, here, :]
                around = (
                    pltpu.roll(value, LANES - 1, 1) * keep_right
                    + pltpu.roll(value, 1, 1) * keep_left
                    + (now[p - 1, here, :] + now[p + 1, here, :])
                    + (now[p, start - 1 : start + 15, :] + now[p, start + 1 : start + 17, :])
                )
                scale, pull, lift, back = table
                inner = around - c[p, here, :] * value
                if lift:
                    inner = inner + (s[p, here, :] if lift == 1.0 else lift * s[p, here, :])
                new = (scale * pull) * value + scale * inner
                if back:
                    new = new - back * target[p, here, :]
                target[p, here, :] = new
        now = target
    row24 = row_iota(24)
    lane24 = lane_iota(24)
    low_row = pl.multiple_of(8 * gz, 8)
    rows_ok = ((row24 >= 8) | (gz > 0)) & ((row24 < 16) | (gz < 7))
    lanes_ok = ((lane24 >= 1) | (gy > 0)) & ((lane24 <= 16) | (gy < 3)) & (lane24 < 18)
    row = lax.broadcasted_iota(jnp.int32, (LANES, LANES), 0)
    column = lax.broadcasted_iota(jnp.int32, (LANES, LANES), 1)
    center = column // 2 + 1
    side = jnp.where(column % 2 == 0, center - 1, center + 1)
    spread = jnp.where(row == center, 0.75, jnp.where(row == side, 0.25, 0.0))
    spread = jnp.where(column < 32, spread, 0.0).astype(F32)
    for j in range(4):
        x = 2 * gx - 1 + j
        x_ok = (x >= 0) & (x < 16)
        xc = jnp.clip(x, 0, 15)
        value = now[1 + xc % 8, pl.ds(low_row, 24), :]
        amount = (2 * LANES - 64 * (xc // 8) - 16 * gy + 1) % LANES
        value = pltpu.roll(value, amount, 1)
        value = jnp.where(rows_ok & lanes_ok & x_ok, value, 0.0)
        window[24 * j : 24 * j + 24, :] = value
    wide = exact_dot(window[...], spread)
    planes = [wide[24 * j : 24 * j + 24, :] for j in range(4)]
    for i in range(4):
        base = i // 2 + 1
        near = base - 1 if i % 2 == 0 else base + 1
        mixed = 0.75 * planes[base] + 0.25 * planes[near]
        window[0:24, :] = mixed
        even = 0.75 * window[8:16, :] + 0.25 * window[7:15, :]
        odd = 0.75 * window[8:16, :] + 0.25 * window[9:17, :]
        window[pl.ds(32, 8, stride=2), :] = even
        window[pl.ds(33, 8, stride=2), :] = odd
        own = rolled(it2[i // 2, :, :], -5 - 64 * (i % 2))
        out[i, :, :] = (own + window[32:48, :])[:, 0:32]


def exchange(low, high, axis):
    return shift(high, axis, 1), shift(low, axis, -1)


def on_device(rs, ab):
    low, high, c1 = call(
        before_kernel,
        [(10, 64, LANES)] * 2 + [(4, 32, LANES)],
        [(64, LANES), (256, LANES)],
        rs, ab,
    )
    fl, fr = exchange(low, high, "gx")
    low, high = call(z_strips_kernel, [(358, LANES)] * 2, [], rs, ab, c1, fl, fr)
    zl, zh = exchange(low, high, "gz")
    es, ec, low, high, c1e = call(
        build0_kernel,
        [(26, 96, LANES)] * 2 + [(288, LANES)] * 2 + [(8, 64, LANES)],
        [],
        rs, ab, c1, fl, fr, zl, zh,
    )
    low0, high0 = exchange(low, high, "gy")
    it0, s1, low, high = call(
        level0_kernel,
        [(16, 64, LANES), (4, 32, LANES)] + [(3, 32, LANES)] * 2,
        [(26, 96, LANES)] * 2 + [(96, LANES)] * 6 + [(80, LANES)] * 3 + [(64, LANES), (256, LANES)],
        es, ec, low, high, low0, high0,
    )
    fl, fr = exchange(low, high, "gx")
    low, high = call(z_strips1_kernel, [(144, LANES)] * 2, [], s1, fl, fr)
    zl, zh = exchange(low, high, "gz")
    ext, low, high = call(
        build1_kernel,
        [(9, 64, LANES)] + [(128, LANES)] * 2,
        [],
        s1, fl, fr, zl, zh,
    )
    yl, yh = exchange(low, high, "gy")
    it1, piece = call(
        level1_kernel,
        [(8, 32, 64), (4, 32, LANES)],
        [(18, 80, LANES)] * 4 + [(64, LANES), (256, LANES)],
        ext, yl, yh, c1e, low0, high0,
    )
    chips = jnp.stack([piece] + [shift(piece, "gx", 2 * k) for k in range(1, 4)])
    others = lax.ppermute(chips, "gx", [(i, i ^ 1) for i in range(8)])
    it2, piece = call(
        level2_kernel,
        [(2, 16, LANES), (2, 8, LANES)],
        [(18, 48, LANES)] * 4 + [(16, LANES), (256, LANES)],
        chips, others,
    )
    near = jnp.stack((piece, shift(piece, "gz", 1), shift(piece, "gz", -1)))
    column = jnp.concatenate((near, shift(near, "gz", 3), shift(near[:2], "gz", -3)))
    grid = jnp.stack([column] + [shift(column, "gy", k) for k in range(1, 4)])
    other = lax.ppermute(grid, "gx", [(i, i ^ 1) for i in range(8)])
    (corrected,) = call(
        bottom_kernel,
        [(4, 16, 32)],
        [(10, 80, LANES)] * 4 + [(96, LANES)],
        grid, other, it2,
    )
    return it0, it1, corrected


def solution(mesh):
    placed = (P("gx", "gz", "gy"), P("gx", "gz", "gy"))
    return jax.shard_map(
        on_device,
        mesh=mesh,
        in_specs=placed,
        out_specs=(P("gx", "gz", "gy"), P("gx", "gz", "gy"), P("gx", "gz", "gy")),
        check_vma=False,
    )
```
